32 devices in a mesh: section: 2 (over x), fsdp: 4 (over z), tp: 4 (over y, core).
Axes of the slice: x: 2, y: 2, z: 4, core: 2. Of those that a mesh axis runs over, the one named last changes fastest.
Arguments:
- inputs: bfloat16 [2, 1024, 1024], P(None, ('fsdp', 'tp')), may hold values from -6 to 6
- segment_ids: int32 [2, 4, 256], P(None, 'fsdp'), may hold values from 0 to 3, never falling along the last dimension, each value on 1 to 128 neighbouring positions
- routes: int32 [2, 2, 1024, 8], P('section', None, 'fsdp'), may hold values from 0 to 31, all different within a row; in each aligned block of 256 rows (0 to 255, 256 to 511, ..., all dimensions but the last counted through in order) at most 128 rows name the same one
- w_query: bfloat16 [2, 1024, 1024], P('section', 'fsdp', 'tp'), may hold values from -0.1875 to 0.1875
- key_weight: bfloat16 [2, 1024, 512], P('section', 'fsdp', 'tp'), may hold values from -0.1875 to 0.1875
- value_weight: bfloat16 [2, 1024, 512], P('section', 'fsdp', 'tp'), may hold values from -0.1875 to 0.1875
- w_output: bfloat16 [2, 1024, 1024], P('section', ('tp', 'fsdp')), may hold values from -1.5 to 1.5
- w_router: bfloat16 [2, 1024, 32], P('section', 'fsdp'), may hold values from -0.375 to 0.375
- gain_attn: float32 [2, 1024], P('section', 'fsdp'), may hold values from 0.5 to 1.5
- gain_moe: float32 [2, 1024], P('section', 'fsdp'), may hold values from 0.5 to 1.5
- w_gate: bfloat16 [2, 32, 1024, 512], P('section', None, 'fsdp', 'tp'), may hold values from -0.1875 to 0.1875
- w_up: bfloat16 [2, 32, 1024, 512], P('section', None, 'fsdp', 'tp'), may hold values from -0.1875 to 0.1875
- w_down: bfloat16 [2, 32, 512, 1024], P('section', None, ('tp', 'fsdp')), may hold values from -1 to 1
- out_grad: bfloat16 [2, 1024, 1024], P(None, ('fsdp', 'tp')), may hold values from -6 to 6
Outputs:
- layer_outputs: bfloat16 [2, 2, 1024, 1024], P('section', None, ('fsdp', 'tp'))
- input_grads: float32 [2, 2, 1024, 1024], P('section', None, ('fsdp', 'tp'))
- w_query_grad: float32 [2, 1024, 1024], P('section', 'fsdp', 'tp')
- w_key_grad: float32 [2, 1024, 512], P('section', 'fsdp', 'tp')
- w_value_grad: float32 [2, 1024, 512], P('section', 'fsdp', 'tp')
- w_output_grad: float32 [2, 1024, 1024], P('section', ('tp', 'fsdp'))
- w_router_grad: float32 [2, 1024, 32], P('section', 'fsdp')
- gain_attn_grad: float32 [2, 1024], P('section', 'fsdp')
- gain_moe_grad: float32 [2, 1024], P('section', 'fsdp')
- w_gate_grad: float32 [2, 32, 1024, 512], P('section', None, 'fsdp', 'tp')
- w_up_grad: float32 [2, 32, 1024, 512], P('section', None, 'fsdp', 'tp')
- w_down_grad: float32 [2, 32, 512, 1024], P('section', None, ('tp', 'fsdp'))
The draws below stay inside these ranges and needn't reach their ends.
Inputs may be any that keep to these rules, and one draw needn't show every extreme that they name: `segment_ids`: within a group the numbers never fall; each sequence has 1 to 128 tokens and one has exactly 128. `routes`: A token names 8 different experts; the 256 tokens of one group name no expert more than 128 times in one layer, a bound that some block reaches.
All inputs are finite; a program needn't handle non-finite values.
Results may differ from the reference program's by a relative error of at most 0.04.
Values may be sent and summed in bfloat16 or wider, within the bound.
A program may use at most 384 MiB of HBM per device.

```python
import math
from functools import partial
import jax
import jax.numpy as jnp
import numpy as np
from jax import lax

MODEL_DIM = 1024
QUERY_HEADS = 16
KEY_VALUE_HEADS = 8
HEAD_SIZE = 64
E = 32
FF = 512
TOP = 8
TOK_DEV = 256
CAP = 128
MICRO = 2
SEG_COUNT = 4
SEGMAX = 128
TOKENS_MB = 1024
N_SECTION = 2
N_FSDP = 4


def shard_levels(own_key, extent, split, low, high):
    loudness = 1.0
    for dim, blocks in split:
        draws = jax.random.uniform(jax.random.fold_in(jax.random.fold_in(own_key, 6), dim), (blocks,), jnp.float32, low / len(split), high / len(split))
        loudness = loudness * jnp.repeat(jnp.exp(draws), extent[dim] // blocks).reshape((-1,) + (1,) * (len(extent) - 1 - dim))
    return loudness


def split_up(count, total, most, lean):
    loads = [(1 << 20) // math.isqrt(standing ** lean) + 1 for standing in range(2, count + 1)]
    rest, given = total - most - (count - 1), [1] * (count - 1)
    while rest > 0:
        candidates = [i for i in range(count - 1) if given[i] < most]
        pool, left = sum([loads[i] for i in candidates]), rest
        for i in candidates:
            more = min(most - given[i], max(1, left * loads[i] // pool), rest)
            given[i] = given[i] + more
            rest = rest - more
    return np.array([most] + given)


def ragged_sizes(stream_key, number_of, total, limit, skew):
    if number_of == 2:
        one = jax.random.randint(stream_key, (), max(1, total - limit), min(limit, total - 1) + 1)
        return jnp.stack([one, total - one])
    tallies = jnp.asarray(split_up(number_of, total, limit, skew), jnp.int32)
    twos = (number_of - 1) // 2
    source_of, sink = tallies[1:1 + 2 * twos:2], tallies[2:2 + 2 * twos:2]
    room = jnp.minimum(source_of - 1, limit - sink)
    shifted = jax.random.randint(jax.random.fold_in(stream_key, 1), (twos,), 0, 1 << 20) % (room + 1)
    tallies = tallies.at[1:1 + 2 * twos:2].set(source_of - shifted).at[2:2 + 2 * twos:2].set(sink + shifted)
    return tallies[jax.random.permutation(jax.random.fold_in(stream_key, 2), number_of)]


def routed_block(stream_key, own, number, rows, number_of, top, most, lean):
    order = jax.random.permutation(stream_key, number_of)
    heavy_load, common = shares(number_of, rows * top, most, lean, True), shares(number_of, rows * top, most, lean, False)
    places = jnp.arange(number_of)

    def named(tallies, offset_by):
        used = int((tallies > 0).sum())
        fixed = max(1, used // 4)
        passed = fixed + (places - fixed + offset_by * (used - fixed)) % max(1, number_of - fixed)
        return jnp.zeros((number_of,), jnp.int32).at[order[jnp.where(places < fixed, places, passed)]].set(jnp.asarray(tallies, jnp.int32))

    tallies = jnp.where(number % 4 == 0, named(heavy_load, number // 4), named(common, number - number // 4 - 1))
    mixed = jax.random.permutation(jax.random.fold_in(own, 3), number_of)
    source_of, sink = mixed[0:number_of // 2 * 2:2], mixed[1:number_of // 2 * 2:2]
    room = jnp.minimum(tallies[source_of] - 1, most - tallies[sink]) // 2
    room = jnp.where((source_of == order[0]) | (sink == order[0]) | (tallies[sink] == 0), 0, jnp.maximum(room, 0))
    passed = jax.random.randint(jax.random.fold_in(own, 4), (number_of // 2,), 0, 1 << 20) % (room + 1)
    tallies = tallies.at[source_of].add(-passed).at[sink].add(passed)
    members = jnp.searchsorted(jnp.cumsum(tallies), jnp.arange(rows * top), side="right").astype(jnp.int32)
    grid = members.reshape(top, rows).T
    grid = grid[jax.random.permutation(jax.random.fold_in(own, 1), rows)]
    offset_by = jax.random.randint(jax.random.fold_in(own, 2), (rows, 1), 0, top)
    return jnp.take_along_axis(grid, (jnp.arange(top)[None, :] + offset_by) % top, axis=1)


def shares(amount, total, most, slope, full):
    portions = [(1 << 20) // math.isqrt(grade ** slope) + 1 for grade in range(1, amount + 1)]
    largest = most if full else min(most, max(-(-total // amount), total * portions[0] // sum(portions)))
    least = 1 if total - largest >= amount - 1 else 0
    counts, spare = [largest] + [least] * (amount - 1), total - largest - least * (amount - 1)
    while spare > 0:
        free = [i for i in range(1, amount) if counts[i] < largest] or [i for i in range(1, amount) if counts[i] < most]
        pool, left = sum([portions[i] for i in free]), spare
        for i in free:
            addition = min(most - counts[i], max(1, left * portions[i] // pool), spare)
            counts[i] = counts[i] + addition
            spare = spare - addition
    return np.array(counts)


def normal_values(stream_key, shape, width, most, cuts=(), kind=jnp.bfloat16):
    values = width * jax.random.normal(stream_key, shape, jnp.float32)
    if cuts:
        values = values * shard_levels(stream_key, shape, cuts, -0.22, 0.18)
    return jnp.clip(values, -most, most).astype(kind)


def setup_inputs(seed: int = 0) -> dict:
    splits = jax.random.split(jax.random.key(seed), 15)
    inputs = normal_values(splits[0], (MICRO, TOKENS_MB, MODEL_DIM), 1.0, 6.0, ((1, 16),))
    segment_ids = jax.vmap(lambda own: jnp.searchsorted(jnp.cumsum(ragged_sizes(own, SEG_COUNT, TOK_DEV, SEGMAX, 1)), jnp.arange(TOK_DEV), side="right"))(jax.random.split(splits[1], MICRO * N_FSDP)).reshape((MICRO, N_FSDP, TOK_DEV)).astype(jnp.int32)
    routes_keys = jax.random.split(jax.random.fold_in(splits[2], 1), N_SECTION * MICRO * TOKENS_MB // TOK_DEV)
    routes_turns = jax.random.permutation(jax.random.fold_in(splits[2], 3), N_SECTION * MICRO * TOKENS_MB // TOK_DEV)
    routes = jax.vmap(lambda own, number: routed_block(jax.random.fold_in(splits[2], 2), own, number, TOK_DEV, E, TOP, CAP, 1))(routes_keys, routes_turns).reshape((N_SECTION, MICRO, TOKENS_MB, TOP))
    w_query = normal_values(splits[3], (N_SECTION, MODEL_DIM, QUERY_HEADS * HEAD_SIZE), MODEL_DIM ** -0.5, 0.1875, ((0, 2), (1, 4), (2, 4)))
    key_weight = normal_values(splits[4], (N_SECTION, MODEL_DIM, KEY_VALUE_HEADS * HEAD_SIZE), MODEL_DIM ** -0.5, 0.1875, ((0, 2), (1, 4), (2, 4)))
    value_weight = normal_values(splits[5], (N_SECTION, MODEL_DIM, KEY_VALUE_HEADS * HEAD_SIZE), MODEL_DIM ** -0.5, 0.1875, ((0, 2), (1, 4), (2, 4)))
    w_output = normal_values(splits[6], (N_SECTION, QUERY_HEADS * HEAD_SIZE, MODEL_DIM), (QUERY_HEADS * HEAD_SIZE // 64) ** -0.5, 1.5, ((0, 2), (1, 16)))
    w_router = normal_values(splits[7], (N_SECTION, MODEL_DIM, E), (MODEL_DIM // 4) ** -0.5, 0.375, ((0, 2), (1, 4)))
    gain_attn = jnp.clip(1.0 + 0.1 * jax.random.normal(splits[8], (N_SECTION, MODEL_DIM), jnp.float32), 0.5, 1.5)
    gain_moe = jnp.clip(1.0 + 0.1 * jax.random.normal(splits[9], (N_SECTION, MODEL_DIM), jnp.float32), 0.5, 1.5)
    w_gate = normal_values(splits[10], (N_SECTION, E, MODEL_DIM, FF), MODEL_DIM ** -0.5, 0.1875, ((0, 2), (2, 4), (3, 4)))
    w_up = normal_values(splits[11], (N_SECTION, E, MODEL_DIM, FF), MODEL_DIM ** -0.5, 0.1875, ((0, 2), (2, 4), (3, 4)))
    w_down = normal_values(splits[12], (N_SECTION, E, FF, MODEL_DIM), (FF // 16) ** -0.5, 1.0, ((0, 2), (2, 16)))
    out_grad = normal_values(splits[13], (MICRO, TOKENS_MB, MODEL_DIM), 1.0, 6.0, ((1, 16),))
    return {"inputs": inputs, "segment_ids": segment_ids, "routes": routes, "w_query": w_query, "key_weight": key_weight, "value_weight": value_weight, "w_output": w_output, "w_router": w_router, "gain_attn": gain_attn, "gain_moe": gain_moe, "w_gate": w_gate, "w_up": w_up, "w_down": w_down, "out_grad": out_grad}


norm_eps = 1e-06
branch_scale = 0.22
score_scale = 0.015625
rope_base = 10000.0
masked_score = -1e+30

def norm_rows(vectors, gain_vec):
    inverse = lax.rsqrt(lax.optimization_barrier(jnp.mean(vectors * vectors, axis=-1, keepdims=True)) + norm_eps)
    normed = vectors * inverse
    return (normed * gain_vec, normed, inverse)

def norm_back(upstream, normed, inverse, gain_vec):
    scaled_grad = upstream * gain_vec
    gain_grad = lax.optimization_barrier(jnp.sum(upstream * normed, axis=0))
    inner_mean = lax.optimization_barrier(jnp.mean(scaled_grad * normed, axis=-1, keepdims=True))
    return (inverse * (scaled_grad - normed * inner_mean), gain_grad)

def rope_tables(segment):
    position = jnp.arange(segment.shape[0], dtype=jnp.int32)
    before = jnp.concatenate([jnp.full((1,), -1, dtype=jnp.int32), segment[:-1].astype(jnp.int32)])
    starts = jnp.where(segment != before, position, jnp.zeros_like(position))
    offsets = (position - lax.cummax(starts, axis=0)).astype(jnp.float32)
    half_dim = HEAD_SIZE // 2
    frequency = rope_base ** (-(jnp.arange(half_dim, dtype=jnp.float32) * 2.0 / HEAD_SIZE))
    angles = offsets[:, None] * frequency[None, :]
    return (jnp.cos(angles)[:, None, :], jnp.sin(angles)[:, None, :])

def rotate(vectors, cosine, sine):
    half_dim = vectors.shape[-1] // 2
    front_half = vectors[..., :half_dim]
    back_half = vectors[..., half_dim:]
    return jnp.concatenate([front_half * cosine - back_half * sine, back_half * cosine + front_half * sine], axis=-1)

def rotate_back(vectors, cosine, sine):
    half_dim = vectors.shape[-1] // 2
    front_half = vectors[..., :half_dim]
    back_half = vectors[..., half_dim:]
    return jnp.concatenate([front_half * cosine + back_half * sine, back_half * cosine - front_half * sine], axis=-1)

def allowed_pairs(segment):
    position = jnp.arange(segment.shape[0], dtype=jnp.int32)
    return (segment[:, None] == segment[None, :]) & (position[None, :] <= position[:, None])

def route_tables(route):
    flat_routes = route.reshape(-1)
    onehot = (flat_routes[:, None] == jnp.arange(E, dtype=jnp.int32)[None, :]).astype(jnp.int32)
    rank_list = lax.optimization_barrier(jnp.sum((jnp.cumsum(onehot, axis=0) - 1) * onehot, axis=1))
    slot_index = (flat_routes * CAP + rank_list).astype(jnp.int32)
    owners = jnp.arange(flat_routes.shape[0], dtype=jnp.int32) // TOP
    source = jnp.zeros((E * CAP,), jnp.int32).at[slot_index].set(owners)
    filled = jnp.zeros((E * CAP,), jnp.int32).at[slot_index].set(jnp.ones_like(owners))
    return (slot_index, source, filled)

def dispatch(rows_in, source, filled):
    picked = jnp.take(rows_in, source, axis=0)
    picked = jnp.where(filled[:, None] == 1, picked, jnp.zeros_like(picked))
    return picked.reshape(E, CAP, rows_in.shape[1])

def collect(slot_rows, slot_index):
    flat_rows = slot_rows.reshape(E * CAP, slot_rows.shape[-1])
    return jnp.take(flat_rows, slot_index, axis=0).reshape(-1, TOP, slot_rows.shape[-1]).sum(axis=1)

def place_shares(route_share, slot_index):
    return jnp.zeros((E * CAP,), jnp.float32).at[slot_index].set(route_share.reshape(-1)).reshape(E, CAP)

def attend(query_rows, key_matrix, value_matrix, permitted_mask):
    scores = jnp.einsum('qhgd,khd->hgqk', query_rows.astype(jnp.float32), key_matrix.astype(jnp.float32)) * score_scale
    scores = jnp.where(permitted_mask[None, None], scores, masked_score)
    row_max = lax.optimization_barrier(jnp.max(scores, axis=-1, keepdims=True))
    log_sum_exp = row_max + jnp.log(lax.optimization_barrier(jnp.sum(jnp.exp(scores - row_max), axis=-1, keepdims=True)))
    weights_low = jnp.exp(scores - log_sum_exp).astype(jnp.bfloat16)
    attended = jnp.einsum('hgqk,khd->qhgd', weights_low.astype(jnp.float32), value_matrix.astype(jnp.float32))
    return (attended.astype(jnp.bfloat16), log_sum_exp)

def attention_backward(query_rows, key_matrix, value_matrix, permitted_mask, log_sum_exp, head_gradient):
    scores = jnp.einsum('qhgd,khd->hgqk', query_rows.astype(jnp.float32), key_matrix.astype(jnp.float32)) * score_scale
    scores = jnp.where(permitted_mask[None, None], scores, masked_score)
    weights_full = jnp.exp(scores - log_sum_exp)
    weights_low = weights_full.astype(jnp.bfloat16)
    heads_wide = head_gradient.astype(jnp.float32)
    value_gradient = jnp.einsum('hgqk,qhgd->khd', weights_low.astype(jnp.float32), heads_wide)
    weight_grad = jnp.einsum('qhgd,khd->hgqk', heads_wide, value_matrix.astype(jnp.float32))
    inner_sum = lax.optimization_barrier(jnp.sum(weights_full * weight_grad, axis=-1, keepdims=True))
    score_grad = (weights_full * (weight_grad - inner_sum) * score_scale).astype(jnp.bfloat16).astype(jnp.float32)
    query_gradient = jnp.einsum('hgqk,khd->qhgd', score_grad, key_matrix.astype(jnp.float32))
    key_gradient = jnp.einsum('hgqk,qhgd->khd', score_grad, query_rows.astype(jnp.float32))
    return (query_gradient, key_gradient, value_gradient)

def experts_forward(routed, slot_share, w_gate, w_up, w_down):
    routed_wide = routed.astype(jnp.float32)
    gate_pre = jnp.einsum('ecd,edf->ecf', routed_wide, w_gate.astype(jnp.float32))
    up_pre = jnp.einsum('ecd,edf->ecf', routed_wide, w_up.astype(jnp.float32))
    hidden = gate_pre * jax.nn.sigmoid(gate_pre) * up_pre
    weighted = (slot_share[:, :, None] * hidden).astype(jnp.bfloat16)
    slot_out = jnp.einsum('ecf,efd->ecd', weighted.astype(jnp.float32), w_down.astype(jnp.float32))
    return (slot_out, gate_pre, up_pre)

def experts_backward(slot_share, gate_pre, up_pre, slot_grad, w_gate, w_up, w_down):
    hidden_grad = jnp.einsum('ecd,efd->ecf', slot_grad.astype(jnp.float32), w_down.astype(jnp.float32))
    sigmoid_gate = jax.nn.sigmoid(gate_pre)
    hidden = gate_pre * sigmoid_gate * up_pre
    share_slot = lax.optimization_barrier(jnp.sum(hidden_grad * hidden, axis=-1))
    scaled_grad = slot_share[:, :, None] * hidden_grad
    gate_grad = (scaled_grad * up_pre * sigmoid_gate * (1.0 + gate_pre * (1.0 - sigmoid_gate))).astype(jnp.bfloat16)
    up_grad = (scaled_grad * gate_pre * sigmoid_gate).astype(jnp.bfloat16)
    routed_grad = jnp.einsum('ecf,edf->ecd', gate_grad.astype(jnp.float32), w_gate.astype(jnp.float32))
    routed_grad = routed_grad + jnp.einsum('ecf,edf->ecd', up_grad.astype(jnp.float32), w_up.astype(jnp.float32))
    weighted = (slot_share[:, :, None] * hidden).astype(jnp.bfloat16)
    return (routed_grad, share_slot, gate_grad, up_grad, weighted)

def layer_forward(layer_in, segment, route, weights):
    w_query, key_weight, value_weight, w_output, w_router, gain_attn, gain_moe, w_gate, w_up, w_down = weights
    count_of_tokens = layer_in.shape[0]
    key_value_heads = key_weight.shape[1] // HEAD_SIZE
    residual = layer_in.astype(jnp.float32)
    scaled_one, normed_one, inverse_one = norm_rows(residual, gain_attn)
    attn_in = scaled_one.astype(jnp.bfloat16)
    cosine, sine = rope_tables(segment)
    permitted_mask = allowed_pairs(segment)
    query_rows = rotate(jnp.dot(attn_in, w_query, preferred_element_type=jnp.float32).reshape(count_of_tokens, -1, HEAD_SIZE), cosine, sine)
    query_rows = query_rows.astype(jnp.bfloat16).reshape(count_of_tokens, key_value_heads, QUERY_HEADS // KEY_VALUE_HEADS, HEAD_SIZE)
    key_matrix = rotate(jnp.dot(attn_in, key_weight, preferred_element_type=jnp.float32).reshape(count_of_tokens, key_value_heads, HEAD_SIZE), cosine, sine).astype(jnp.bfloat16)
    value_matrix = jnp.dot(attn_in, value_weight, preferred_element_type=jnp.float32).astype(jnp.bfloat16).reshape(count_of_tokens, key_value_heads, HEAD_SIZE)
    attended, log_sum_exp = attend(query_rows, key_matrix, value_matrix, permitted_mask)
    mixed_heads = attended.reshape(count_of_tokens, -1)
    hidden_state = residual + branch_scale * jnp.dot(mixed_heads, w_output, preferred_element_type=jnp.float32)
    scaled_two, normed_two, inverse_two = norm_rows(hidden_state, gain_moe)
    moe_in = scaled_two.astype(jnp.bfloat16)
    logits = jnp.dot(moe_in, w_router, preferred_element_type=jnp.float32)
    route_share = jax.nn.softmax(jnp.take_along_axis(logits, route, axis=1), axis=-1)
    slot_index, source, filled = route_tables(route)
    slot_share = place_shares(route_share, slot_index)
    routed = dispatch(moe_in, source, filled)
    slot_out, gate_pre, up_pre = experts_forward(routed, slot_share, w_gate, w_up, w_down)
    result = (hidden_state + branch_scale * collect(slot_out, slot_index)).astype(jnp.bfloat16)
    kept_state = (attn_in, query_rows, key_matrix, value_matrix, attended, log_sum_exp, normed_one, inverse_one, normed_two, inverse_two, moe_in, route_share, slot_share, slot_index, source, filled, gate_pre, up_pre, cosine, sine, permitted_mask, route, routed)
    return (result, kept_state)

def layer_backward(upstream, kept_state, weights):
    w_query, key_weight, value_weight, w_output, w_router, gain_attn, gain_moe, w_gate, w_up, w_down = weights
    attn_in, query_rows, key_matrix, value_matrix, attended, log_sum_exp, normed_one, inverse_one, normed_two, inverse_two, moe_in, route_share, slot_share, slot_index, source, filled, gate_pre, up_pre, cosine, sine, permitted_mask, route, routed = kept_state
    count_of_tokens = upstream.shape[0]
    key_value_heads = key_matrix.shape[1]
    moe_grad = (branch_scale * upstream).astype(jnp.bfloat16)
    slot_grad = dispatch(moe_grad, source, filled)
    routed_grad, share_slot, gate_grad, up_grad, weighted = experts_backward(slot_share, gate_pre, up_pre, slot_grad, w_gate, w_up, w_down)
    routed_wide = routed.astype(jnp.float32)
    gate_w = jnp.einsum('ecd,ecf->edf', routed_wide, gate_grad.astype(jnp.float32))
    up_w = jnp.einsum('ecd,ecf->edf', routed_wide, up_grad.astype(jnp.float32))
    down_w = jnp.einsum('ecf,ecd->efd', weighted.astype(jnp.float32), slot_grad.astype(jnp.float32))
    token_grad = collect(routed_grad, slot_index)
    share_grad = jnp.take(share_slot.reshape(-1), slot_index).reshape(count_of_tokens, TOP)
    chosen_grad = route_share * (share_grad - lax.optimization_barrier(jnp.sum(route_share * share_grad, axis=-1, keepdims=True)))
    onehot = (route[:, :, None] == jnp.arange(E, dtype=jnp.int32)[None, None, :]).astype(jnp.float32)
    logit_grad = jnp.einsum('tr,tre->te', chosen_grad, onehot).astype(jnp.bfloat16)
    router_w = jnp.einsum('td,te->de', moe_in.astype(jnp.float32), logit_grad.astype(jnp.float32))
    norm_grad = token_grad + jnp.dot(logit_grad, w_router.T, preferred_element_type=jnp.float32)
    back_two, gain_two = norm_back(norm_grad, normed_two, inverse_two, gain_moe)
    hidden_grad = upstream + back_two
    attn_grad = (branch_scale * hidden_grad).astype(jnp.bfloat16)
    mixed_heads = attended.reshape(count_of_tokens, -1)
    head_gradient = jnp.dot(attn_grad, w_output.T, preferred_element_type=jnp.float32).astype(jnp.bfloat16)
    output_w = jnp.einsum('tk,td->kd', mixed_heads.astype(jnp.float32), attn_grad.astype(jnp.float32))
    query_gradient, key_gradient, value_gradient = attention_backward(query_rows, key_matrix, value_matrix, permitted_mask, log_sum_exp, head_gradient.reshape(count_of_tokens, key_value_heads, QUERY_HEADS // KEY_VALUE_HEADS, HEAD_SIZE))
    query_gradient = rotate_back(query_gradient.reshape(count_of_tokens, -1, HEAD_SIZE), cosine, sine).reshape(count_of_tokens, -1).astype(jnp.bfloat16)
    key_gradient = rotate_back(key_gradient, cosine, sine).reshape(count_of_tokens, -1).astype(jnp.bfloat16)
    value_gradient = value_gradient.reshape(count_of_tokens, -1).astype(jnp.bfloat16)
    attn_wide = attn_in.astype(jnp.float32)
    query_w = jnp.einsum('td,tk->dk', attn_wide, query_gradient.astype(jnp.float32))
    key_w = jnp.einsum('td,tk->dk', attn_wide, key_gradient.astype(jnp.float32))
    value_w = jnp.einsum('td,tk->dk', attn_wide, value_gradient.astype(jnp.float32))
    input_part = jnp.dot(query_gradient, w_query.T, preferred_element_type=jnp.float32)
    input_part = input_part + jnp.dot(key_gradient, key_weight.T, preferred_element_type=jnp.float32)
    input_part = input_part + jnp.dot(value_gradient, value_weight.T, preferred_element_type=jnp.float32)
    back_one, gain_one = norm_back(input_part, normed_one, inverse_one, gain_attn)
    return (hidden_grad + back_one, (query_w, key_w, value_w, output_w, router_w, gain_one, gain_two, gate_w, up_w, down_w))

def forward_only(group_item, weights):
    layer_in, segment, route = group_item
    return layer_forward(layer_in, segment, route, weights)[0]

def reference(inputs, segment_ids, routes, w_query, key_weight, value_weight, w_output, w_router, gain_attn, gain_moe, w_gate, w_up, w_down, out_grad):
    groups = MICRO * N_FSDP
    segments = segment_ids.reshape(groups, TOK_DEV)
    weight_sets = [tuple((matrix[layer_index] for matrix in (w_query, key_weight, value_weight, w_output, w_router, gain_attn, gain_moe, w_gate, w_up, w_down))) for layer_index in range(N_SECTION)]
    current = inputs.reshape(groups, TOK_DEV, MODEL_DIM)
    layer_inputs = []
    outputs_list = []
    for layer_index in range(N_SECTION):
        layer_inputs.append(current)
        route_set = routes[layer_index].reshape(groups, TOK_DEV, TOP)
        current = lax.map(partial(forward_only, weights=weight_sets[layer_index]), (current, segments, route_set))
        outputs_list.append(current)
    upstream = out_grad.reshape(groups, TOK_DEV, MODEL_DIM).astype(jnp.float32)
    grads_list = [None] * N_SECTION
    input_list = [None] * N_SECTION
    for layer_index in reversed(range(N_SECTION)):
        weights = weight_sets[layer_index]
        route_set = routes[layer_index].reshape(groups, TOK_DEV, TOP)
        totals = tuple((jnp.zeros(matrix.shape, jnp.float32) for matrix in weights))

        def group_step(running, group_item, weights=weights):
            layer_in, segment, route, grad_rows = group_item
            kept_state = layer_forward(layer_in, segment, route, weights)[1]
            grad_out, grads = layer_backward(grad_rows, kept_state, weights)
            return (jax.tree.map(jnp.add, running, grads), grad_out)
        totals, upstream = lax.scan(group_step, totals, (layer_inputs[layer_index], segments, route_set, upstream))
        grads_list[layer_index] = totals
        input_list[layer_index] = upstream
    layer_outputs = jnp.stack(outputs_list).reshape(N_SECTION, MICRO, TOKENS_MB, MODEL_DIM)
    input_grads = jnp.stack(input_list).reshape(N_SECTION, MICRO, TOKENS_MB, MODEL_DIM)
    stacked = [jnp.stack([grads_list[layer_index][which] for layer_index in range(N_SECTION)]) for which in range(10)]
    return (layer_outputs, input_grads, stacked[0], stacked[1], stacked[2], stacked[3], stacked[4], stacked[5], stacked[6], stacked[7], stacked[8], stacked[9])
```

```python
import jax
import jax.numpy as jnp
from jax import lax
from jax.sharding import PartitionSpec as P

QUERY_HEADS = 16
KEY_VALUE_HEADS = 8
HEAD_SIZE = 64


norm_eps = 1e-06
branch_scale = 0.22
score_scale = 0.015625
rope_base = 10000.0
masked_score = -1e30


def from_behind(array, axis, by):
    count = lax.axis_size(axis)
    pairs = [(i, i + by) for i in range(count) if 0 <= i + by < count]
    return lax.ppermute(array, axis, pairs)


def shortened(array):
    return jax.tree.map(lambda a: a.astype(jnp.bfloat16) if a.dtype == jnp.float32 else a, array)


def norm_rows(vectors, gain_vec):
    inverse = lax.rsqrt(jnp.mean(vectors * vectors, axis=-1, keepdims=True) + norm_eps)
    normed = vectors * inverse
    return (normed * gain_vec, normed, inverse)


def norm_back(upstream, normed, inverse, gain_vec):
    scaled_grad = upstream * gain_vec
    gain_grad = jnp.sum(upstream * normed, axis=0)
    inner_mean = jnp.mean(scaled_grad * normed, axis=-1, keepdims=True)
    return (inverse * (scaled_grad - normed * inner_mean), gain_grad)


def rope_tables(permitted_mask):
    offsets = (jnp.sum(permitted_mask.astype(jnp.int32), axis=1) - 1).astype(jnp.float32)
    half_dim = HEAD_SIZE // 2
    frequency = rope_base ** (-(jnp.arange(half_dim, dtype=jnp.float32) * 2.0 / HEAD_SIZE))
    angles = offsets[:, None] * frequency[None, :]
    return (jnp.cos(angles)[:, None, :], jnp.sin(angles)[:, None, :])


def rotate(vectors, cosine, sine):
    half_dim = vectors.shape[-1] // 2
    front_half = vectors[..., :half_dim]
    back_half = vectors[..., half_dim:]
    return jnp.concatenate(
        [front_half * cosine - back_half * sine, back_half * cosine + front_half * sine], axis=-1
    )


def rotate_back(vectors, cosine, sine):
    half_dim = vectors.shape[-1] // 2
    front_half = vectors[..., :half_dim]
    back_half = vectors[..., half_dim:]
    return jnp.concatenate(
        [front_half * cosine + back_half * sine, back_half * cosine - front_half * sine], axis=-1
    )


def allowed_pairs(segment):
    position = jnp.arange(segment.shape[0], dtype=jnp.int32)
    return (segment[:, None] == segment[None, :]) & (position[None, :] <= position[:, None])


def attend(query_rows, key_matrix, value_matrix, permitted_mask):
    scores = (
        jnp.einsum("qhgd,khd->hgqk", query_rows, key_matrix, preferred_element_type=jnp.float32)
        * score_scale
    )
    scores = jnp.where(permitted_mask[None, None], scores, masked_score)
    row_max = jnp.max(scores, axis=-1, keepdims=True)
    log_sum_exp = row_max + jnp.log(jnp.sum(jnp.exp(scores - row_max), axis=-1, keepdims=True))
    weights_low = jnp.exp(scores - log_sum_exp).astype(jnp.bfloat16)
    attended = jnp.einsum(
        "hgqk,khd->qhgd", weights_low, value_matrix, preferred_element_type=jnp.float32
    )
    return (attended.astype(jnp.bfloat16), log_sum_exp)


def attention_backward(
    query_rows, key_matrix, value_matrix, permitted_mask, log_sum_exp, head_gradient
):
    scores = (
        jnp.einsum("qhgd,khd->hgqk", query_rows, key_matrix, preferred_element_type=jnp.float32)
        * score_scale
    )
    scores = jnp.where(permitted_mask[None, None], scores, masked_score)
    weights_full = jnp.exp(scores - log_sum_exp)
    weights_low = weights_full.astype(jnp.bfloat16)
    value_gradient = jnp.einsum(
        "hgqk,qhgd->khd", weights_low, head_gradient, preferred_element_type=jnp.float32
    )
    weight_grad = jnp.einsum(
        "qhgd,khd->hgqk", head_gradient, value_matrix, preferred_element_type=jnp.float32
    )
    inner_sum = jnp.sum(weights_full * weight_grad, axis=-1, keepdims=True)
    score_grad = (weights_full * (weight_grad - inner_sum) * score_scale).astype(jnp.bfloat16)
    query_gradient = jnp.einsum(
        "hgqk,khd->qhgd", score_grad, key_matrix, preferred_element_type=jnp.float32
    )
    key_gradient = jnp.einsum(
        "hgqk,qhgd->khd", score_grad, query_rows, preferred_element_type=jnp.float32
    )
    return (query_gradient, key_gradient, value_gradient)


GROUP = ("fsdp", "tp")


def exchange(blocks):
    return lax.all_to_all(blocks, "fsdp", split_axis=0, concat_axis=0, tiled=True)


def expert_matrices(w_gate, w_up, w_down):
    count = lax.axis_size("fsdp")
    experts, depth, hidden_units = w_gate.shape
    local = experts // count
    pair = jnp.stack([w_gate, w_up], axis=0).reshape(2, count, local, depth, hidden_units)
    pair = exchange(pair.transpose(1, 3, 0, 2, 4).reshape(count, depth, -1))
    gate_up = pair.reshape(count * depth, 2 * local * hidden_units)
    down = exchange(w_down.reshape(count, local, w_down.shape[1], w_down.shape[2]))
    down = down.transpose(1, 0, 2, 3).reshape(local * hidden_units, w_down.shape[2])
    return (gate_up, down)


def expert_shards(both_w, down_w, local, hidden_units):
    count = lax.axis_size("fsdp")
    both = exchange(both_w.reshape(count, -1, both_w.shape[1]))
    depth = both.shape[1]
    both = both.reshape(count, depth, 2, local, hidden_units).transpose(2, 0, 3, 1, 4)
    both = both.reshape(2, count * local, depth, hidden_units).astype(jnp.float32)
    down = down_w.reshape(local, count, hidden_units // count, -1).transpose(1, 0, 2, 3)
    down = exchange(down).reshape(count * local, hidden_units // count, -1).astype(jnp.float32)
    return (both[0], both[1], down)


def spread(shares, hidden_units):
    rows, local = shares.shape
    wide = jnp.broadcast_to(shares[:, :, None], (rows, local, hidden_units))
    return wide.reshape(rows, local * hidden_units)


def forward_layer(layer_in, segment, chosen, weights, own):
    w_qkv, w_output, w_router, gain_attn, gain_moe, gate_up, w_down = weights
    first, local = own
    query_width = w_output.shape[0]
    key_width = (w_qkv.shape[1] - query_width) // 2
    key_value_heads = key_width // HEAD_SIZE
    hidden_units = w_down.shape[0] // local
    residual = layer_in.astype(jnp.float32)
    scaled_one, normed_one, inverse_one = norm_rows(residual, gain_attn)
    attn_in = lax.all_gather(scaled_one.astype(jnp.bfloat16), "tp", axis=0, tiled=True)
    count_of_tokens = attn_in.shape[0]
    permitted_mask = allowed_pairs(segment)
    cosine, sine = rope_tables(permitted_mask)
    qkv = jnp.dot(attn_in, w_qkv, preferred_element_type=jnp.float32)
    turned = rotate(
        qkv[:, : query_width + key_width].reshape(count_of_tokens, -1, HEAD_SIZE), cosine, sine
    ).astype(jnp.bfloat16)
    query_rows = turned[:, : query_width // HEAD_SIZE].reshape(
        count_of_tokens, key_value_heads, QUERY_HEADS // KEY_VALUE_HEADS, HEAD_SIZE
    )
    key_matrix = turned[:, query_width // HEAD_SIZE :]
    value_matrix = (
        qkv[:, query_width + key_width :]
        .astype(jnp.bfloat16)
        .reshape(count_of_tokens, key_value_heads, HEAD_SIZE)
    )
    attended, log_sum_exp = attend(query_rows, key_matrix, value_matrix, permitted_mask)
    mixed_heads = attended.reshape(count_of_tokens, -1)
    attn_out = lax.psum_scatter(
        jnp.dot(mixed_heads, w_output, preferred_element_type=jnp.float32).astype(jnp.bfloat16),
        "tp",
        scatter_dimension=0,
        tiled=True,
    ).astype(jnp.float32)
    hidden_state = residual + branch_scale * attn_out
    scaled_two, normed_two, inverse_two = norm_rows(hidden_state, gain_moe)
    own_rows = scaled_two.astype(jnp.bfloat16)
    moe_in = lax.all_gather(own_rows, GROUP, axis=0, tiled=True)
    logits = jnp.dot(moe_in, w_router, preferred_element_type=jnp.float32)
    logits = jnp.where(chosen, logits, masked_score)
    share = jax.nn.softmax(logits, axis=-1)
    share = jnp.where(chosen, share, 0.0)
    slot_share = lax.dynamic_slice_in_dim(share, first, local, 1)
    both_pre = jnp.dot(moe_in, gate_up, preferred_element_type=jnp.float32)
    half = both_pre.shape[1] // 2
    gate_pre = both_pre[:, :half]
    up_pre = both_pre[:, half:]
    hidden = gate_pre * jax.nn.sigmoid(gate_pre) * up_pre
    weighted = (spread(slot_share, hidden_units) * hidden).astype(jnp.bfloat16)
    combined = jnp.dot(weighted, w_down, preferred_element_type=jnp.float32)
    moe_out = lax.psum_scatter(
        combined.astype(jnp.bfloat16), GROUP, scatter_dimension=0, tiled=True
    ).astype(jnp.float32)
    result = (hidden_state + branch_scale * moe_out).astype(jnp.bfloat16)
    kept_state = (
        attn_in,
        query_rows,
        key_matrix,
        value_matrix,
        attended,
        log_sum_exp,
        normed_one,
        inverse_one,
        normed_two,
        inverse_two,
        own_rows,
        moe_in,
        share,
        slot_share,
        both_pre,
        weighted,
        cosine,
        sine,
        permitted_mask,
    )
    return (result, kept_state)


def backward_layer(upstream, kept_state, weights, own):
    w_qkv, w_output, w_router, gain_attn, gain_moe, gate_up, w_down = weights
    first, local = own
    (
        attn_in,
        query_rows,
        key_matrix,
        value_matrix,
        attended,
        log_sum_exp,
        normed_one,
        inverse_one,
        normed_two,
        inverse_two,
        own_rows,
        moe_in,
        share,
        slot_share,
        both_pre,
        weighted,
        cosine,
        sine,
        permitted_mask,
    ) = kept_state
    local_rows = upstream.shape[0]
    count_of_tokens = attn_in.shape[0]
    key_value_heads = key_matrix.shape[1]
    hidden_units = w_down.shape[0] // local
    place = lax.axis_index("fsdp") * lax.axis_size("tp") + lax.axis_index("tp")
    moe_grad = lax.all_gather(
        (branch_scale * upstream).astype(jnp.bfloat16), GROUP, axis=0, tiled=True
    )
    hidden_grad = lax.dot_general(
        moe_grad, w_down, (((1,), (1,)), ((), ())), preferred_element_type=jnp.float32
    )
    half = both_pre.shape[1] // 2
    gate_pre = both_pre[:, :half]
    up_pre = both_pre[:, half:]
    sigmoid_gate = jax.nn.sigmoid(gate_pre)
    hidden = gate_pre * sigmoid_gate * up_pre
    share_part = jnp.sum(
        (hidden_grad * hidden).reshape(moe_grad.shape[0], local, hidden_units), axis=-1
    )
    share_wide = lax.dynamic_update_slice_in_dim(jnp.zeros_like(share), share_part, first, 1)
    share_grad = lax.psum_scatter(share_wide, GROUP, scatter_dimension=0, tiled=True)
    scaled_grad = spread(slot_share, hidden_units) * hidden_grad
    gate_grad = (
        scaled_grad * up_pre * sigmoid_gate * (1.0 + gate_pre * (1.0 - sigmoid_gate))
    ).astype(jnp.bfloat16)
    up_grad = (scaled_grad * gate_pre * sigmoid_gate).astype(jnp.bfloat16)
    both_grad = jnp.concatenate([gate_grad, up_grad], axis=-1)
    token_grad = lax.dot_general(
        both_grad, gate_up, (((1,), (1,)), ((), ())), preferred_element_type=jnp.float32
    )
    norm_grad = lax.psum_scatter(
        token_grad.astype(jnp.bfloat16), GROUP, scatter_dimension=0, tiled=True
    ).astype(jnp.float32)
    own_share = lax.dynamic_slice_in_dim(share, place * local_rows, local_rows, 0)
    logit_grad = (
        own_share * (share_grad - jnp.sum(own_share * share_grad, axis=-1, keepdims=True))
    ).astype(jnp.bfloat16)
    norm_grad = norm_grad + jnp.dot(logit_grad, w_router.T, preferred_element_type=jnp.float32)
    back_two, gain_two = norm_back(norm_grad, normed_two, inverse_two, gain_moe)
    state_grad = upstream + back_two
    attn_grad = lax.all_gather(
        (branch_scale * state_grad).astype(jnp.bfloat16), "tp", axis=0, tiled=True
    )
    mixed_heads = attended.reshape(count_of_tokens, -1)
    head_gradient = jnp.dot(attn_grad, w_output.T, preferred_element_type=jnp.float32).astype(
        jnp.bfloat16
    )
    query_gradient, key_gradient, value_gradient = attention_backward(
        query_rows,
        key_matrix,
        value_matrix,
        permitted_mask,
        log_sum_exp,
        head_gradient.reshape(
            count_of_tokens, key_value_heads, QUERY_HEADS // KEY_VALUE_HEADS, HEAD_SIZE
        ),
    )
    turned = jnp.concatenate(
        [query_gradient.reshape(count_of_tokens, -1, HEAD_SIZE), key_gradient], axis=1
    )
    turned = rotate_back(turned, cosine, sine).reshape(count_of_tokens, -1)
    qkv_grad = jnp.concatenate(
        [turned, value_gradient.reshape(count_of_tokens, -1)], axis=1
    ).astype(jnp.bfloat16)
    input_part = lax.dot_general(
        qkv_grad, w_qkv, (((1,), (1,)), ((), ())), preferred_element_type=jnp.float32
    )
    norm_one_grad = lax.psum_scatter(
        input_part.astype(jnp.bfloat16), "tp", scatter_dimension=0, tiled=True
    ).astype(jnp.float32)
    back_one, gain_one = norm_back(norm_one_grad, normed_one, inverse_one, gain_attn)
    terms = (
        (attn_in, qkv_grad),
        (mixed_heads, attn_grad),
        (logit_grad, own_rows),
        (moe_in, both_grad),
        (weighted, moe_grad),
    )
    return (state_grad + back_one, (gain_one, gain_two), terms)


def summed_product(pairs):
    left = jnp.concatenate([pair[0] for pair in pairs], axis=0)
    right = jnp.concatenate([pair[1] for pair in pairs], axis=0)
    return lax.dot_general(
        left, right, (((0,), (0,)), ((), ())), preferred_element_type=jnp.float32
    )


def per_device(
    inputs,
    segment_ids,
    routes,
    w_query,
    key_weight,
    value_weight,
    w_output,
    w_router,
    gain_attn,
    gain_moe,
    w_gate,
    w_up,
    w_down,
    out_grad,
):
    section_count = lax.axis_size("section")
    section_index = lax.axis_index("section")
    fsdp_count = lax.axis_size("fsdp")
    micro_count = inputs.shape[0]
    local_rows = inputs.shape[1]
    model_width = inputs.shape[2]
    depth = w_query.shape[1]
    expert_count = w_router.shape[2]
    local = expert_count // fsdp_count
    hidden_units = w_gate.shape[3]
    query_width = w_query.shape[2]
    key_width = key_weight.shape[2]
    qkv_width = query_width + 2 * key_width
    flat_output = w_output[0].reshape(depth, -1)
    output_width = flat_output.shape[1]
    packed = jnp.concatenate(
        [
            w_query[0],
            key_weight[0],
            value_weight[0],
            flat_output,
            w_router[0],
            gain_attn[0].astype(jnp.bfloat16)[:, None],
            gain_moe[0].astype(jnp.bfloat16)[:, None],
        ],
        axis=1,
    )
    packed = lax.all_gather(packed, "fsdp", axis=0, tiled=True)
    after = qkv_width + output_width
    gate_up, down_full = expert_matrices(w_gate[0], w_up[0], w_down[0])
    weights = (
        packed[:, :qkv_width],
        packed[:, qkv_width:after].reshape(-1, model_width),
        packed[:, after : after + expert_count],
        packed[:, after + expert_count].astype(jnp.float32),
        packed[:, after + expert_count + 1].astype(jnp.float32),
        gate_up,
        down_full,
    )
    expert_ids = jnp.arange(expert_count, dtype=jnp.int32)
    chosen_rows = jnp.any(routes[0][..., None] == expert_ids, axis=2).astype(jnp.bfloat16)
    chosen_rows = lax.all_gather(chosen_rows, "fsdp", axis=1, tiled=True)
    own = (lax.axis_index("fsdp") * local, local)
    segment_rows = segment_ids[:, 0, :]
    tick_count = micro_count + section_count - 1
    outputs = jnp.zeros((micro_count, local_rows, model_width), jnp.bfloat16)
    history = []
    previous = None
    for tick_step in range(tick_count):
        mb_index = tick_step - section_index
        active = (mb_index >= 0) & (mb_index < micro_count)
        mb_pick = jnp.clip(mb_index, 0, micro_count - 1)
        fresh_input = inputs[min(tick_step, micro_count - 1)]
        if previous is None:
            arrived = jnp.zeros_like(fresh_input)
        else:
            arrived = from_behind(previous, "section", 1)
        layer_in = jnp.where(section_index == 0, fresh_input, arrived)
        segment = lax.dynamic_index_in_dim(segment_rows, mb_pick, 0, keepdims=False)
        chosen = lax.dynamic_index_in_dim(chosen_rows, mb_pick, 0, keepdims=False) > 0.5
        result, kept_state = forward_layer(layer_in, segment, chosen, weights, own)
        outputs = jnp.where(
            active, lax.dynamic_update_index_in_dim(outputs, result, mb_pick, 0), outputs
        )
        history.append(kept_state)
        previous = result
    input_grads = jnp.zeros((micro_count, local_rows, model_width), jnp.float32)
    gain_sums = None
    all_terms = []
    previous = None
    for tick_step in range(tick_count):
        mb_index = micro_count + section_count - 2 - tick_step - section_index
        active = (mb_index >= 0) & (mb_index < micro_count)
        mb_pick = jnp.clip(mb_index, 0, micro_count - 1)
        fresh_grad = out_grad[max(micro_count - 1 - tick_step, 0)].astype(jnp.float32)
        if previous is None:
            arrived = jnp.zeros_like(fresh_grad)
        else:
            arrived = from_behind(shortened(previous), "section", -1).astype(previous.dtype)
        upstream = jnp.where(section_index == section_count - 1, fresh_grad, arrived)
        upstream = jnp.where(active, upstream, jnp.zeros_like(upstream))
        grad_out, gains, terms = backward_layer(
            upstream, history[tick_count - 1 - tick_step], weights, own
        )
        input_grads = jnp.where(
            active, lax.dynamic_update_index_in_dim(input_grads, grad_out, mb_pick, 0), input_grads
        )
        gain_sums = gains if gain_sums is None else tuple(a + b for a, b in zip(gain_sums, gains))
        all_terms.append(terms)
        previous = grad_out
    qkv_pairs, output_pairs, router_pairs, both_pairs, down_pairs = zip(*all_terms)
    both_w = summed_product(both_pairs).astype(jnp.bfloat16)
    down_w = summed_product(down_pairs).astype(jnp.bfloat16)
    gate_shard, up_shard, down_shard = expert_shards(both_w, down_w, local, hidden_units)
    small = jnp.concatenate([summed_product(router_pairs), jnp.stack(gain_sums)], axis=0)
    small = lax.psum(small, "tp").T
    packed_grad = jnp.concatenate(
        [
            summed_product(qkv_pairs),
            summed_product(output_pairs).reshape(model_width, -1),
            small,
        ],
        axis=1,
    ).astype(jnp.bfloat16)
    packed_grad = lax.psum_scatter(
        packed_grad, "fsdp", scatter_dimension=0, tiled=True
    ).astype(jnp.float32)
    shard_sums = (
        packed_grad[:, :query_width],
        packed_grad[:, query_width : query_width + key_width],
        packed_grad[:, query_width + key_width : qkv_width],
        packed_grad[:, qkv_width:after].reshape(-1, model_width),
        packed_grad[:, after : after + expert_count],
        packed_grad[:, after + expert_count],
        packed_grad[:, after + expert_count + 1],
        gate_shard,
        up_shard,
        down_shard,
    )
    return (outputs[None], input_grads[None]) + tuple((part[None] for part in shard_sums))


def solution(mesh):
    in_specs = (
        P(None, ("fsdp", "tp"), None),
        P(None, "fsdp", None),
        P("section", None, "fsdp", None),
        P("section", "fsdp", "tp"),
        P("section", "fsdp", "tp"),
        P("section", "fsdp", "tp"),
        P("section", ("tp", "fsdp"), None),
        P("section", "fsdp", None),
        P("section", "fsdp"),
        P("section", "fsdp"),
        P("section", None, "fsdp", "tp"),
        P("section", None, "fsdp", "tp"),
        P("section", None, ("tp", "fsdp"), None),
        P(None, ("fsdp", "tp"), None),
    )
    out_specs = (
        P("section", None, ("fsdp", "tp"), None),
        P("section", None, ("fsdp", "tp"), None),
        P("section", "fsdp", "tp"),
        P("section", "fsdp", "tp"),
        P("section", "fsdp", "tp"),
        P("section", ("tp", "fsdp"), None),
        P("section", "fsdp", None),
        P("section", "fsdp"),
        P("section", "fsdp"),
        P("section", None, "fsdp", "tp"),
        P("section", None, "fsdp", "tp"),
        P("section", None, ("tp", "fsdp"), None),
    )
    return jax.shard_map(
        per_device, mesh=mesh, in_specs=in_specs, out_specs=out_specs, check_vma=False
    )
```
